32 devices in a mesh: blk: 16 (over z, y, x), col: 2 (over core).
Axes of the slice: x: 2, y: 2, z: 4, core: 2. Of those that a mesh axis runs over, the one named last changes fastest.
Arguments:
- queries: bfloat16 [128, 16384], P('blk', 'col'), may hold values from -6 to 6
- factor: bfloat16 [16384, 1024], P('col', 'blk'), may hold values from -0.046875 to 0.046875
- eigenvalues: float32 [1024], replicated, may hold values from 0.05 to 20
- damping: float32 [1], replicated, may hold values from 0.5 to 2
- train_rows: bfloat16 [16384, 16384], P('blk', 'col'), may hold values from -0.046875 to 0.046875
Outputs:
- scores: bfloat16 [128, 16384], P('col', 'blk')
The draws below stay inside these ranges and needn't reach their ends.
All inputs are finite; a program needn't handle non-finite values.
Results may differ from the reference program's by a relative error of at most 0.0049.
Values may be sent and summed in bfloat16 or wider, within the bound.
A program may use at most 64 MiB of HBM per device.

```python
import math
import jax
import jax.numpy as jnp
from jax import lax

PROJ = 16384
RANK = 1024
TR_DEV = 1024
QUERIES = 128
TRAIN = 16384
N_BLK = 16


def block_scale(key, dims, shards, smallest, high):
    loudness = 1.0
    for position, shards_of in shards:
        heights = jax.random.uniform(jax.random.fold_in(jax.random.fold_in(key, 6), position), (shards_of,), jnp.float32, smallest / len(shards), high / len(shards))
        loudness = loudness * jnp.repeat(jnp.exp(heights), dims[position] // shards_of).reshape((-1,) + (1,) * (len(dims) - 1 - position))
    return loudness


def centred(rng, dims, deviation, most, shards=(), dtype=jnp.bfloat16):
    level = block_scale(rng, dims, shards, -0.22, 0.18) if shards else 1.0
    array = jax.random.normal(rng, dims, jnp.float32) * deviation * level
    return jnp.minimum(jnp.maximum(array, -most), most).astype(dtype)


def setup_inputs(seed: int = 0) -> dict:
    key_of = jax.random.split(jax.random.key(seed), 6)
    return {
        "queries": centred(key_of[0], (QUERIES, PROJ), 1.0, 6.0, ((0, 16), (1, 2))),
        "factor": centred(key_of[1], (PROJ, RANK), PROJ ** -0.5, 0.046875, ((0, 2), (1, 16))),
        "eigenvalues": jnp.clip(jnp.exp(jax.random.uniform(key_of[2], (RANK,), jnp.float32, math.log(0.05), math.log(20.0))), 0.05, 20.0),
        "damping": jnp.clip(jnp.exp(jax.random.uniform(key_of[3], (1,), jnp.float32, math.log(0.5), math.log(2.0))), 0.5, 2.0),
        "train_rows": centred(key_of[4], (TRAIN, PROJ), PROJ ** -0.5, 0.046875, ((0, 16), (1, 2))),
    }


def reference(queries, factor, eigenvalues, damping, train_rows):
    damp_value = damping[0]
    weights = eigenvalues / (eigenvalues + damp_value)
    coefficient = jnp.dot(queries, factor, preferred_element_type=jnp.float32)
    scaled = coefficient * weights[None, :]
    correction = jnp.dot(scaled, factor.astype(jnp.float32).T, precision=lax.Precision.HIGHEST)
    preconditioned = ((queries.astype(jnp.float32) - correction) / damp_value).astype(jnp.bfloat16)
    blocks = train_rows.reshape(N_BLK, TR_DEV, PROJ)

    def one_block(block_rows):
        return jnp.dot(preconditioned, block_rows.T, preferred_element_type=jnp.float32).astype(jnp.bfloat16)

    result = lax.map(one_block, blocks)
    return jnp.transpose(result, (1, 0, 2)).reshape(QUERIES, TRAIN)
```

```python
import functools

import jax
import jax.numpy as jnp
from jax import lax
from jax.experimental import pallas as pl
from jax.experimental.pallas import tpu as pltpu
from jax.sharding import PartitionSpec as P

MESH = pl.DeviceIdType.MESH
CONTRACT_LAST = (((1,), (1,)), ((), ()))


def fused_kernel(
    nb, queries, factor_t, eigenvalues, damping, train_rows, out,
    query_out, factor_out, query_in, factor_in, train_in, part, pair_in, sum_in, scaled,
    terms_out, terms_in, own_terms, pre, total, total_in,
    train_sem, load_sem, query_send, query_recv, factor_send, factor_recv,
    rows_send, rows_recv, sum_send, sum_recv, terms_send, terms_recv,
    line_send, line_recv, side_send, side_recv, corner_send, corner_recv, pair_send, pair_recv,
):
    me = lax.axis_index("blk")
    side = lax.axis_index("col")
    rows, depth = queries.shape
    plane_size = 4
    line = nb // plane_size
    wide = depth // plane_size
    width = wide // line
    piece = width // 2
    every = nb * rows
    half = every // 2
    rank_slice = factor_t.shape[0]
    plane_rank = plane_size * rank_slice
    px, py, pz = lax.rem(me, 2), lax.rem(lax.div(me, 2), 2), lax.div(me, 4)
    z_low, z_high = lax.rem(pz, 2), lax.div(pz, 2)

    def flip(bit, yes):
        return 1 - bit if yes else bit

    def spot(k):
        return flip(px, k & 1) + 2 * flip(py, k & 2)

    def height_at(d):
        return flip(z_low, d & 1) + 2 * flip(z_high, d & 2)

    def chip(d, k):
        return height_at(d) * plane_size + spot(k)

    def span(index, size):
        return pl.ds(pl.multiple_of(index * size, size), size)

    def to_chip(source, target, send_sem, recv_sem, peer):
        return pltpu.make_async_remote_copy(
            src_ref=source, dst_ref=target, send_sem=send_sem, recv_sem=recv_sem,
            device_id={"blk": peer}, device_id_type=MESH,
        )

    def to_pair(source, target, index):
        return pltpu.make_async_remote_copy(
            src_ref=source, dst_ref=target,
            send_sem=pair_send.at[index], recv_sem=pair_recv.at[index],
            device_id={"col": 1 - side}, device_id_type=MESH,
        )

    def load_query(k):
        target = query_out.at[k - 1] if k else query_in.at[me]
        return pltpu.make_async_copy(queries.at[:, span(spot(k), wide)], target, load_sem.at[0, k])

    def load_factor(k):
        target = factor_out.at[k - 1] if k else factor_in.at[spot(0)]
        return pltpu.make_async_copy(factor_t.at[:, span(spot(k), wide)], target, load_sem.at[1, k])

    def query_copy(k, source):
        return to_chip(query_out.at[k - 1], query_in.at[source],
                       query_send.at[k - 1], query_recv.at[k - 1], chip(0, k))

    def factor_copy(k, source):
        return to_chip(factor_out.at[k - 1], factor_in.at[source],
                       factor_send.at[k - 1], factor_recv.at[k - 1], chip(0, k))

    def rows_copy(d, k, source):
        return to_chip(query_in.at[source], query_in.at[source],
                       rows_send.at[d - 1, k], rows_recv.at[d - 1, k], chip(d, 0))

    def sum_copy(k):
        return to_chip(part, sum_in.at[k - 1], sum_send.at[k - 1], sum_recv.at[k - 1], chip(0, k))

    def terms_copy(d, k):
        return to_chip(terms_out.at[d - 1, k], terms_in.at[d - 1, k],
                       terms_send.at[d - 1, k], terms_recv.at[d - 1, k], chip(d, 0))

    def block(z, flip_x, flip_y):
        return z * plane_size + flip(py, flip_y) * 2 + flip(px, flip_x)

    def piece_of(index, k):
        return pre.at[index, :, pl.ds(k * piece, piece)]

    def line_copy(z, k, up):
        ref = piece_of(block(z, False, False), k)
        return to_chip(ref, ref, line_send.at[up, 2 * z + k], line_recv.at[2 * z + k],
                       me + (plane_size if up else -plane_size))

    next_x, next_y = chip(0, 1), chip(0, 2)

    def side_copy(z, k, along, incoming=False):
        ref = piece_of(block(z, incoming and along == 0, incoming and along == 1), k)
        return to_chip(ref, ref, side_send.at[along, 2 * z + k], side_recv.at[along, 2 * z + k],
                       next_y if along else next_x)

    def corner_copy(z, along, incoming=False):
        ref = piece_of(block(z, incoming or along == 1, incoming or along == 0), 1 - along)
        return to_chip(ref, ref, corner_send.at[along, z], corner_recv.at[along, z],
                       next_y if along else next_x)

    def train_copy(index):
        z, place = lax.div(index, plane_size), lax.rem(index, plane_size)
        return pltpu.make_async_copy(
            train_rows.at[:, span(place * line + z, width)], train_in.at[index], train_sem.at[index])

    for k in range(plane_size):
        load_query(k).start()
    for k in (3, 1, 2, 0):
        load_factor(k).start()

    barrier = pltpu.get_barrier_semaphore()
    for k in range(1, plane_size):
        pl.semaphore_signal(barrier, inc=1, device_id={"blk": chip(0, k)}, device_id_type=MESH)
    for d in range(1, line):
        pl.semaphore_signal(barrier, inc=1, device_id={"blk": chip(d, 0)}, device_id_type=MESH)
    pl.semaphore_signal(barrier, inc=1, device_id={"col": 1 - side}, device_id_type=MESH)
    pl.semaphore_wait(barrier, plane_size + line - 1)

    for k in (3, 1, 2):
        load_query(k).wait()
        query_copy(k, me).start()
    for k in (3, 1, 2):
        load_factor(k).wait()
        factor_copy(k, spot(0)).start()
    load_query(0).wait()
    for d in (2, 3, 1):
        rows_copy(d, 0, me).start()

    def start_train(k, carry):
        train_copy(lax.rem(me + nb - k, nb)).start()
        return carry
    lax.fori_loop(0, nb, start_train, 0)

    for k in range(1, plane_size):
        query_copy(k, chip(0, k)).wait_recv()
        for d in (2, 3, 1):
            rows_copy(d, k, chip(0, k)).start()
    load_factor(0).wait()
    for k in (1, 2, 3):
        factor_copy(k, spot(k)).wait_recv()
    for d in range(1, line):
        for k in range(plane_size):
            rows_copy(d, k, chip(d, k)).wait_recv()

    query_wide = query_in[...].astype(jnp.float32).reshape(every, wide).astype(jnp.bfloat16)
    partial_value = lax.dot_general(
        query_wide, factor_in[...].reshape(plane_rank, wide),
        CONTRACT_LAST, preferred_element_type=jnp.float32)
    part[...] = partial_value

    own_values = eigenvalues[:, span(pz, plane_rank)]
    weights = own_values / (own_values + damping[0])

    @pl.when(side == 0)
    def _():
        to_pair(part, pair_in, 0).start()
        to_pair(scaled, scaled, 1).wait_recv()
        to_pair(part, pair_in, 0).wait_send()

    @pl.when(side == 1)
    def _():
        to_pair(part, pair_in, 0).wait_recv()
        part[...] = part[...] + pair_in[...]
        for k in (3, 1, 2):
            sum_copy(k).start()
        for k in (1, 2, 3):
            sum_copy(k).wait_recv()
        whole = ((part[...] + sum_in[0]) + (sum_in[1] + sum_in[2])) * weights
        first = whole.astype(jnp.bfloat16)
        scaled[0:every] = first
        scaled[every:2 * every] = (whole - first.astype(jnp.float32)).astype(jnp.bfloat16)
        to_pair(scaled, scaled, 1).start()

    def terms_of(z):
        both = jnp.dot(scaled[...], factor_in[:, :, span(z, width)].reshape(plane_rank, width),
                       preferred_element_type=jnp.float32)
        return both[:every] + both[every:]

    for d in (3, 2, 1):
        terms = terms_of(height_at(d)).astype(jnp.bfloat16)
        for k in range(2):
            terms_out[d - 1, k] = terms[:, k * piece:(k + 1) * piece]
            terms_copy(d, k).start()
    own_terms[...] = terms_of(pz)
    inverse = 1.0 / damping[0]

    def finish_own(k):
        for d in (1, 2, 3):
            terms_copy(d, k).wait_recv()
        whole = own_terms[:, k * piece:(k + 1) * piece] + (
            (terms_in[0, k].astype(jnp.float32) + terms_in[1, k].astype(jnp.float32))
            + terms_in[2, k].astype(jnp.float32))
        start = pl.multiple_of(pz * width + k * piece, piece)
        own = query_in[:, :, pl.ds(start, piece)].astype(jnp.float32).reshape(every, piece)
        pre[me, :, k * piece:(k + 1) * piece] = ((own - whole) * inverse).astype(jnp.bfloat16)

    def scores_of(index):
        train_copy(index).wait()
        return lax.dot_general(
            pre[index], train_in[index], CONTRACT_LAST, preferred_element_type=jnp.float32)

    def height(i):
        mirror = lax.div(pz, line // 2)
        near = pz + mirror * (line - 1 - 2 * pz)
        v = near + i * (1 - 2 * near) if i < 2 else i
        return v + mirror * (line - 1 - 2 * v)

    def pass_on(z, k):
        @pl.when((z <= pz) & (pz < line - 1))
        def _():
            line_copy(z, k, 1).start()

        @pl.when((z >= pz) & (pz > 0))
        def _():
            line_copy(z, k, 0).start()

    total[...] = jnp.zeros_like(total)
    side_lag, corner_lag = 3, 6

    def add_scores(z, flip_x, flip_y):
        total[...] += scores_of(block(z, flip_x, flip_y))

    for e in range(2 * line + corner_lag):
        if e < 2 * line:
            i, k = divmod(e, 2)
            z = height(i)
            if i > 0:
                line_copy(z, k, 1).wait_recv()
            else:
                finish_own(k)
            pass_on(z, k)
            side_copy(z, k, 0).start()
            side_copy(z, k, 1).start()
        if 0 <= e - side_lag < 2 * line:
            i, k = divmod(e - side_lag, 2)
            z = height(i)
            side_copy(z, k, k, True).wait_recv()
            corner_copy(z, 1 - k).start()
            if k == 1:
                side_copy(z, 1, 0, True).wait_recv()
                add_scores(z, True, False)
                side_copy(z, 0, 1, True).wait_recv()
                add_scores(z, False, True)
        if e < 2 * line and e % 2 == 1:
            add_scores(height(e // 2), False, False)
        if e >= corner_lag:
            i, k = divmod(e - corner_lag, 2)
            z = height(i)
            corner_copy(z, 1 - k, True).wait_recv()
            if k == 1:
                add_scores(z, True, True)

    other_rows = pl.ds(pl.multiple_of((1 - side) * half, half), half)
    own_rows = pl.ds(pl.multiple_of(side * half, half), half)
    last = to_pair(total.at[other_rows], total_in, 2)
    last.start()

    for k in range(1, plane_size):
        query_copy(k, me).wait_send()
        factor_copy(k, spot(0)).wait_send()
    for d in range(1, line):
        for k in range(plane_size):
            rows_copy(d, k, chip(0, k)).wait_send()
        for k in range(2):
            terms_copy(d, k).wait_send()

    @pl.when(side == 1)
    def _():
        for k in range(1, plane_size):
            sum_copy(k).wait_send()
        to_pair(scaled, scaled, 1).wait_send()

    for i in range(line):
        z = height(i)
        for k in range(2):
            @pl.when((z <= pz) & (pz < line - 1))
            def _():
                line_copy(z, k, 1).wait_send()

            @pl.when((z >= pz) & (pz > 0))
            def _():
                line_copy(z, k, 0).wait_send()

            for along in range(2):
                side_copy(z, k, along).wait_send()
        for along in range(2):
            corner_copy(z, along).wait_send()
    last.wait()
    out[...] = (total[own_rows, :] + total_in[...]).astype(out.dtype)


def fused(nb, queries, factor, eigenvalues, damping, train_rows):
    rows, depth = queries.shape
    rank_slice = factor.shape[1]
    plane_size = 4
    line = nb // plane_size
    wide = depth // plane_size
    width = wide // line
    every = nb * rows
    train = train_rows.shape[0]
    plane_rank = plane_size * rank_slice
    anywhere = pl.BlockSpec(memory_space=pl.ANY)
    vmem = pl.BlockSpec(memory_space=pltpu.VMEM)
    dma = pltpu.SemaphoreType.DMA
    f32, bf16 = jnp.float32, jnp.bfloat16
    return pl.pallas_call(
        functools.partial(fused_kernel, nb),
        out_shape=jax.ShapeDtypeStruct((every // 2, train), bf16),
        in_specs=[anywhere, anywhere, vmem, pl.BlockSpec(memory_space=pltpu.SMEM), anywhere],
        out_specs=vmem,
        scratch_shapes=[
            pltpu.VMEM((plane_size - 1, rows, wide), bf16),
            pltpu.VMEM((plane_size - 1, rank_slice, wide), bf16),
            pltpu.VMEM((nb, rows, wide), bf16),
            pltpu.VMEM((plane_size, rank_slice, wide), bf16),
            pltpu.VMEM((nb, train, width), bf16),
            pltpu.VMEM((every, plane_rank), f32),
            pltpu.VMEM((every, plane_rank), f32),
            pltpu.VMEM((plane_size - 1, every, plane_rank), f32),
            pltpu.VMEM((2 * every, plane_rank), bf16),
            pltpu.VMEM((line - 1, 2, every, width // 2), bf16),
            pltpu.VMEM((line - 1, 2, every, width // 2), bf16),
            pltpu.VMEM((every, width), f32),
            pltpu.VMEM((nb, every, width), bf16),
            pltpu.VMEM((every, train), f32),
            pltpu.VMEM((every // 2, train), f32),
            dma((nb,)), dma((2, plane_size)),
            dma((plane_size - 1,)), dma((plane_size - 1,)),
            dma((plane_size - 1,)), dma((plane_size - 1,)),
            dma((line - 1, plane_size)), dma((line - 1, plane_size)),
            dma((plane_size - 1,)), dma((plane_size - 1,)),
            dma((line - 1, 2)), dma((line - 1, 2)),
            dma((2, 2 * line)), dma((2 * line,)), dma((2, 2 * line)), dma((2, 2 * line)),
            dma((2, line)), dma((2, line)), dma((3,)), dma((3,)),
        ],
        compiler_params=pltpu.CompilerParams(
            collective_id=0, has_side_effects=True, vmem_limit_bytes=56 * 1024 * 1024),
    )(queries, factor.T, eigenvalues[None, :], damping, train_rows)


def plain(queries, factor, eigenvalues, damping, train_rows):
    damp_value = damping[0]
    weights = eigenvalues / (eigenvalues + damp_value)
    query_part = lax.all_to_all(queries, "blk", split_axis=1, concat_axis=0, tiled=True)
    factor_part = lax.all_to_all(factor, "blk", split_axis=0, concat_axis=1, tiled=True)
    partial_value = jnp.dot(query_part, factor_part, preferred_element_type=jnp.float32)
    coefficient = lax.psum(partial_value, ("blk", "col"))
    scaled = coefficient * weights[None, :]
    correction = jnp.dot(scaled, factor_part.astype(jnp.float32).T, precision=lax.Precision.HIGHEST)
    pre_part = ((query_part.astype(jnp.float32) - correction) / damp_value).astype(jnp.bfloat16)
    pre_all = lax.all_gather(pre_part, "blk", axis=1, tiled=True)
    partial_scores = jnp.einsum("qk,nk->qn", pre_all, train_rows, preferred_element_type=jnp.float32)
    scores = lax.psum_scatter(partial_scores, "col", scatter_dimension=0, tiled=True)
    return scores.astype(jnp.bfloat16)


def per_device(nb, pair, queries, factor, eigenvalues, damping, train_rows):
    rows, depth = queries.shape
    width = depth // nb
    fits = pair == 2 and width % 256 == 0 and eigenvalues.shape[0] % 512 == 0 and rows % 8 == 0 and factor.shape[1] % 16 == 0
    fits = fits and nb == 16
    if fits:
        return fused(nb, queries, factor, eigenvalues, damping, train_rows)
    return plain(queries, factor, eigenvalues, damping, train_rows)


def solution(mesh):
    in_specs = (P("blk", "col"), P("col", "blk"), P(), P(), P("blk", "col"))
    out_specs = P("col", "blk")
    body = functools.partial(per_device, mesh.shape["blk"], mesh.shape["col"])
    return jax.shard_map(
        body, mesh=mesh, in_specs=in_specs, out_specs=out_specs, check_vma=False
    )
```

```python
import functools

import jax
import jax.numpy as jnp
from jax import lax
from jax.experimental import pallas as pl
from jax.experimental.pallas import tpu as pltpu
from jax.sharding import PartitionSpec as P

MESH = pl.DeviceIdType.MESH
CONTRACT_LAST = (((1,), (1,)), ((), ()))


def fused_kernel(
    nb, queries, factor_t, eigenvalues, damping, train_rows, out,
    query_out, factor_out, query_in, factor_in, near_factor, train_in, part, pair_in, sum_in, scaled,
    terms, terms_out, terms_in, pre, total, total_in,
    train_sem, load_sem, query_send, query_recv, factor_send, factor_recv, near_send, near_recv,
    rows_send, rows_recv, sum_send, sum_recv, scaled_send, scaled_recv, terms_send, terms_recv,
    line_send, line_recv, far_send, side_send, side_recv, corner_send, corner_recv, pair_send, pair_recv,
):
    me = lax.axis_index("blk")
    side = lax.axis_index("col")
    rows, depth = queries.shape
    plane_size = 4
    line = nb // plane_size
    wide = depth // plane_size
    width = wide // line
    piece = width // 2
    every = nb * rows
    half = every // 2
    rank_slice = factor_t.shape[0]
    plane_rank = plane_size * rank_slice
    px, py, pz = lax.rem(me, 2), lax.rem(lax.div(me, 2), 2), lax.div(me, 4)
    z_low, z_high = lax.rem(pz, 2), lax.div(pz, 2)

    def flip(bit, yes):
        return 1 - bit if yes else bit

    def spot(k):
        return flip(px, k & 1) + 2 * flip(py, k & 2)

    def height_at(d):
        return flip(z_low, d & 1) + 2 * flip(z_high, d & 2)

    def chip(d, k):
        return height_at(d) * plane_size + spot(k)

    def span(index, size):
        return pl.ds(pl.multiple_of(index * size, size), size)

    def to_chip(source, target, send_sem, recv_sem, peer):
        return pltpu.make_async_remote_copy(
            src_ref=source, dst_ref=target, send_sem=send_sem, recv_sem=recv_sem,
            device_id={"blk": peer}, device_id_type=MESH,
        )

    def to_pair(source, target, index):
        return pltpu.make_async_remote_copy(
            src_ref=source, dst_ref=target,
            send_sem=pair_send.at[index], recv_sem=pair_recv.at[index],
            device_id={"col": 1 - side}, device_id_type=MESH,
        )

    def load_query(k):
        target = query_out.at[k - 1] if k else query_in.at[me]
        return pltpu.make_async_copy(queries.at[:, span(spot(k), wide)], target, load_sem.at[0, k])

    def load_factor(k):
        target = factor_out.at[k - 1] if k else factor_in.at[spot(0)]
        return pltpu.make_async_copy(factor_t.at[:, span(spot(k), wide)], target, load_sem.at[1, k])

    def query_copy(k, source):
        return to_chip(query_out.at[k - 1], query_in.at[source],
                       query_send.at[k - 1], query_recv.at[k - 1], chip(0, k))

    def factor_copy(k, source):
        return to_chip(factor_out.at[k - 1], factor_in.at[source],
                       factor_send.at[k - 1], factor_recv.at[k - 1], chip(0, k))

    def rows_copy(d, k, source):
        return to_chip(query_in.at[source], query_in.at[source],
                       rows_send.at[d - 1, k], rows_recv.at[d - 1, k], chip(d, 0))

    def sum_copy(k):
        return to_chip(part, sum_in.at[k - 1], sum_send.at[k - 1], sum_recv.at[k - 1], chip(0, k))

    def near_copy(part_index, k):
        columns = span(height_at(3 if part_index else 1), width)
        return to_chip(factor_in.at[spot(k), :, columns], near_factor.at[part_index, spot(k)],
                       near_send.at[part_index, k], near_recv.at[part_index, k], chip(1, 0))

    def scaled_copy(core):
        return pltpu.make_async_remote_copy(
            src_ref=scaled.at[0], dst_ref=scaled.at[1],
            send_sem=scaled_send.at[core], recv_sem=scaled_recv.at[0],
            device_id={"blk": chip(1, 0), "col": core}, device_id_type=MESH)

    def terms_copy(k):
        return to_chip(terms_out.at[k], terms_in.at[k], terms_send.at[k], terms_recv.at[k], chip(2, 0))

    def block(z, flip_x, flip_y):
        return z * plane_size + flip(py, flip_y) * 2 + flip(px, flip_x)

    def piece_of(index, k):
        return pre.at[index, :, pl.ds(k * piece, piece)]

    def line_copy(z, k, up):
        ref = piece_of(block(z, False, False), k)
        return to_chip(ref, ref, line_send.at[up, 2 * z + k], line_recv.at[2 * z + k],
                       me + (plane_size if up else -plane_size))

    next_x, next_y = chip(0, 1), chip(0, 2)

    def side_copy(z, k, along, incoming=False):
        ref = piece_of(block(z, incoming and along == 0, incoming and along == 1), k)
        return to_chip(ref, ref, side_send.at[along, 2 * z + k], side_recv.at[along, 2 * z + k],
                       next_y if along else next_x)

    def corner_copy(z, along, incoming=False):
        ref = piece_of(block(z, incoming or along == 1, incoming or along == 0), 1 - along)
        return to_chip(ref, ref, corner_send.at[along, z], corner_recv.at[along, z],
                       next_y if along else next_x)

    def train_copy(index):
        z, place = lax.div(index, plane_size), lax.rem(index, plane_size)
        return pltpu.make_async_copy(
            train_rows.at[:, span(place * line + z, width)], train_in.at[index], train_sem.at[index])

    for k in range(plane_size):
        load_query(k).start()
    for k in (3, 1, 2, 0):
        load_factor(k).start()

    barrier = pltpu.get_barrier_semaphore()
    for k in range(1, plane_size):
        pl.semaphore_signal(barrier, inc=1, device_id={"blk": chip(0, k)}, device_id_type=MESH)
    for d in range(1, line):
        pl.semaphore_signal(barrier, inc=1, device_id={"blk": chip(d, 0)}, device_id_type=MESH)
    pl.semaphore_signal(barrier, inc=1, device_id={"col": 1 - side}, device_id_type=MESH)
    pl.semaphore_signal(
        barrier, inc=1, device_id={"blk": chip(1, 0), "col": 1 - side}, device_id_type=MESH)
    pl.semaphore_wait(barrier, plane_size + line)

    for k in (3, 1, 2):
        load_query(k).wait()
        query_copy(k, me).start()
    for k in (3, 1, 2):
        load_factor(k).wait()
        factor_copy(k, spot(0)).start()
    load_query(0).wait()
    for d in (2, 3, 1):
        rows_copy(d, 0, me).start()
    load_factor(0).wait()
    for part_index in (1, 0):
        near_copy(part_index, 0).start()

    def start_train(k, carry):
        train_copy(lax.rem(me + nb - k, nb)).start()
        return carry
    lax.fori_loop(0, nb, start_train, 0)

    for k in range(1, plane_size):
        query_copy(k, chip(0, k)).wait_recv()
        for d in (2, 3, 1):
            rows_copy(d, k, chip(0, k)).start()
    for k in (1, 2, 3):
        factor_copy(k, spot(k)).wait_recv()
        for part_index in (1, 0):
            near_copy(part_index, k).start()
    for d in range(1, line):
        for k in range(plane_size):
            rows_copy(d, k, chip(d, k)).wait_recv()

    query_wide = query_in[...].astype(jnp.float32).reshape(every, wide).astype(jnp.bfloat16)
    partial_value = lax.dot_general(
        query_wide, factor_in[...].reshape(plane_rank, wide),
        CONTRACT_LAST, preferred_element_type=jnp.float32)
    part[...] = partial_value

    own_values = eigenvalues[:, span(pz, plane_rank)]
    weights = own_values / (own_values + damping[0])

    @pl.when(side == 0)
    def _():
        to_pair(part, pair_in, 0).start()
        to_pair(scaled.at[0], scaled.at[0], 1).wait_recv()
        to_pair(part, pair_in, 0).wait_send()

    @pl.when(side == 1)
    def _():
        to_pair(part, pair_in, 0).wait_recv()
        part[...] = part[...] + pair_in[...]
        for k in (3, 1, 2):
            sum_copy(k).start()
        for k in (1, 2, 3):
            sum_copy(k).wait_recv()
        whole = ((part[...] + sum_in[0]) + (sum_in[1] + sum_in[2])) * weights
        first = whole.astype(jnp.bfloat16)
        scaled[0, 0:every] = first
        scaled[0, every:2 * every] = (whole - first.astype(jnp.float32)).astype(jnp.bfloat16)
        scaled_copy(0).start()
        to_pair(scaled.at[0], scaled.at[0], 1).start()
        scaled_copy(1).start()

    parts = ((1, 0), (1, 1), (0, 0), (0, 1))

    def product(which, factor_part):
        both = jnp.dot(scaled[which], factor_part.reshape(plane_rank, piece),
                       preferred_element_type=jnp.float32)
        return both[:every] + both[every:]

    for part_index, k in parts:
        columns = span(2 * height_at(2 * part_index) + k, piece)
        terms[part_index, k] = product(0, factor_in[:, :, columns])
    for part_index in (1, 0):
        for k in range(plane_size):
            near_copy(part_index, k).wait_recv()
    scaled_copy(0).wait_recv()
    for part_index, k in parts:
        near_part = near_factor[part_index, :, :, k * piece:(k + 1) * piece]
        whole = terms[part_index, k] + product(1, near_part)
        if part_index:
            terms_out[k] = whole.astype(jnp.bfloat16)
            terms_copy(k).start()
        else:
            terms[part_index, k] = whole
    inverse = 1.0 / damping[0]

    def finish_own(k):
        terms_copy(k).wait_recv()
        whole = terms[0, k] + terms_in[k].astype(jnp.float32)
        start = pl.multiple_of(pz * width + k * piece, piece)
        own = query_in[:, :, pl.ds(start, piece)].astype(jnp.float32).reshape(every, piece)
        pre[me, :, k * piece:(k + 1) * piece] = ((own - whole) * inverse).astype(jnp.bfloat16)

    def scores_of(index):
        train_copy(index).wait()
        return lax.dot_general(
            pre[index], train_in[index], CONTRACT_LAST, preferred_element_type=jnp.float32)

    def height(i):
        mirror = lax.div(pz, line // 2)
        near = pz + mirror * (line - 1 - 2 * pz)
        v = near + i * (1 - 2 * near) if i < 2 else i
        return v + mirror * (line - 1 - 2 * v)

    def pass_on(z, k):
        @pl.when((z <= pz) & (pz < line - 1))
        def _():
            line_copy(z, k, 1).start()

        @pl.when((z >= pz) & (pz > 0))
        def _():
            line_copy(z, k, 0).start()

    total[...] = jnp.zeros_like(total)
    def add_scores(z, flip_x, flip_y):
        total[...] += scores_of(block(z, flip_x, flip_y))

    direct_line, direct_corner = (True, False), (((3, 1),), ())

    def for_cores(chosen, body, otherwise=None):
        if chosen[0] == chosen[1]:
            if chosen[0]:
                body()
            elif otherwise:
                otherwise()
            return
        pl.when(side == (1 if chosen[1] else 0))(body)
        if otherwise:
            pl.when(side == (0 if chosen[1] else 1))(otherwise)

    def far_copy(d, k):
        ref = piece_of(me, k)
        return to_chip(ref, ref, far_send.at[d - 1, k], line_recv.at[2 * pz + k], chip(d, 0))

    def diagonal_copy(z, k):
        ref = piece_of(block(z, False, False), k)
        return to_chip(ref, ref, corner_send.at[1 - k, z], corner_recv.at[1 - k, z], chip(0, 3))

    def at_corner(i, k):
        return tuple((i, k) in direct_corner[core] for core in range(2))

    def start_line(i, k):
        def direct():
            if i == 0:
                for d in (3, 2, 1):
                    far_copy(d, k).start()
        for_cores(direct_line, direct, lambda: pass_on(height(i), k))

    def line_sent(i, k):
        z = height(i)

        def direct():
            if i == 0:
                for d in (3, 2, 1):
                    far_copy(d, k).wait_send()

        def relayed():
            @pl.when((z <= pz) & (pz < line - 1))
            def _():
                line_copy(z, k, 1).wait_send()

            @pl.when((z >= pz) & (pz > 0))
            def _():
                line_copy(z, k, 0).wait_send()
        for_cores(direct_line, direct, relayed)

    def arrive(i, k):
        z = height(i)
        if i > 0:
            line_copy(z, k, 1).wait_recv()
        else:
            finish_own(k)
        start_line(i, k)
        for_cores(at_corner(i, k), lambda: diagonal_copy(z, k).start())
        side_copy(z, k, k).start()

    def spread(i, k):
        side_copy(height(i), k, 1 - k).start()

    def turn(i, k):
        z = height(i)
        side_copy(z, k, k, True).wait_recv()
        for_cores(at_corner(i, k), lambda: None, lambda: corner_copy(z, 1 - k).start())

    def add_own(i):
        add_scores(height(i), False, False)

    def add_side(i, along):
        z = height(i)
        side_copy(z, 1 - along, along, True).wait_recv()
        add_scores(z, along == 0, along == 1)

    def add_corner(i):
        z = height(i)
        for along in range(2):
            corner_copy(z, along, True).wait_recv()
        add_scores(z, True, True)

    arrive(0, 0)
    spread(0, 0)
    arrive(0, 1)
    spread(0, 1)
    add_own(0)
    arrive(1, 0)
    spread(1, 0)
    arrive(1, 1)
    spread(1, 1)
    turn(0, 0)
    add_own(1)
    arrive(2, 0)
    spread(2, 0)
    turn(0, 1)
    add_side(0, 0)
    add_side(0, 1)
    arrive(2, 1)
    spread(2, 1)
    turn(1, 0)
    add_own(2)
    arrive(3, 0)
    spread(3, 0)
    turn(1, 1)
    add_side(1, 0)
    add_side(1, 1)
    arrive(3, 1)
    spread(3, 1)
    turn(2, 0)
    add_own(3)
    add_corner(0)
    turn(2, 1)
    add_side(2, 0)
    add_side(2, 1)
    turn(3, 0)
    add_corner(1)
    turn(3, 1)
    add_side(3, 0)
    add_side(3, 1)
    add_corner(2)
    add_corner(3)
    other_rows = pl.ds(pl.multiple_of((1 - side) * half, half), half)
    own_rows = pl.ds(pl.multiple_of(side * half, half), half)
    last = to_pair(total.at[other_rows], total_in, 2)
    last.start()

    for k in range(1, plane_size):
        query_copy(k, me).wait_send()
        factor_copy(k, spot(0)).wait_send()
    for d in range(1, line):
        for k in range(plane_size):
            rows_copy(d, k, chip(0, k)).wait_send()
    for k in range(plane_size):
        for part_index in range(2):
            near_copy(part_index, k).wait_send()
    for k in range(2):
        terms_copy(k).wait_send()

    @pl.when(side == 1)
    def _():
        for k in range(1, plane_size):
            sum_copy(k).wait_send()
        to_pair(scaled.at[0], scaled.at[0], 1).wait_send()
        for core in range(2):
            scaled_copy(core).wait_send()

    for i in range(line):
        z = height(i)
        for k in range(2):
            line_sent(i, k)
            for along in range(2):
                side_copy(z, k, along).wait_send()
        for along in range(2):
            corner_copy(z, along).wait_send()
    last.wait()
    out[...] = (total[own_rows, :] + total_in[...]).astype(out.dtype)


def fused(nb, queries, factor, eigenvalues, damping, train_rows):
    rows, depth = queries.shape
    rank_slice = factor.shape[1]
    plane_size = 4
    line = nb // plane_size
    wide = depth // plane_size
    width = wide // line
    every = nb * rows
    train = train_rows.shape[0]
    plane_rank = plane_size * rank_slice
    anywhere = pl.BlockSpec(memory_space=pl.ANY)
    vmem = pl.BlockSpec(memory_space=pltpu.VMEM)
    dma = pltpu.SemaphoreType.DMA
    f32, bf16 = jnp.float32, jnp.bfloat16
    return pl.pallas_call(
        functools.partial(fused_kernel, nb),
        out_shape=jax.ShapeDtypeStruct((every // 2, train), bf16),
        in_specs=[anywhere, anywhere, vmem, pl.BlockSpec(memory_space=pltpu.SMEM), anywhere],
        out_specs=vmem,
        scratch_shapes=[
            pltpu.VMEM((plane_size - 1, rows, wide), bf16),
            pltpu.VMEM((plane_size - 1, rank_slice, wide), bf16),
            pltpu.VMEM((nb, rows, wide), bf16),
            pltpu.VMEM((plane_size, rank_slice, wide), bf16),
            pltpu.VMEM((2, plane_size, rank_slice, width), bf16),
            pltpu.VMEM((nb, train, width), bf16),
            pltpu.VMEM((every, plane_rank), f32),
            pltpu.VMEM((every, plane_rank), f32),
            pltpu.VMEM((plane_size - 1, every, plane_rank), f32),
            pltpu.VMEM((2, 2 * every, plane_rank), bf16),
            pltpu.VMEM((2, 2, every, width // 2), f32),
            pltpu.VMEM((2, every, width // 2), bf16),
            pltpu.VMEM((2, every, width // 2), bf16),
            pltpu.VMEM((nb, every, width), bf16),
            pltpu.VMEM((every, train), f32),
            pltpu.VMEM((every // 2, train), f32),
            dma((nb,)), dma((2, plane_size)),
            dma((plane_size - 1,)), dma((plane_size - 1,)),
            dma((plane_size - 1,)), dma((plane_size - 1,)),
            dma((2, plane_size)), dma((2, plane_size)),
            dma((line - 1, plane_size)), dma((line - 1, plane_size)),
            dma((plane_size - 1,)), dma((plane_size - 1,)),
            dma((2,)), dma((1,)), dma((2,)), dma((2,)),
            dma((2, 2 * line)), dma((2 * line,)), dma((line - 1, 2)), dma((2, 2 * line)), dma((2, 2 * line)),
            dma((2, line)), dma((2, line)), dma((3,)), dma((3,)),
        ],
        compiler_params=pltpu.CompilerParams(
            collective_id=0, has_side_effects=True, vmem_limit_bytes=55040 * 1024),
    )(queries, factor.T, eigenvalues[None, :], damping, train_rows)


def plain(queries, factor, eigenvalues, damping, train_rows):
    damp_value = damping[0]
    weights = eigenvalues / (eigenvalues + damp_value)
    query_part = lax.all_to_all(queries, "blk", split_axis=1, concat_axis=0, tiled=True)
    factor_part = lax.all_to_all(factor, "blk", split_axis=0, concat_axis=1, tiled=True)
    partial_value = jnp.dot(query_part, factor_part, preferred_element_type=jnp.float32)
    coefficient = lax.psum(partial_value, ("blk", "col"))
    scaled = coefficient * weights[None, :]
    correction = jnp.dot(scaled, factor_part.astype(jnp.float32).T, precision=lax.Precision.HIGHEST)
    pre_part = ((query_part.astype(jnp.float32) - correction) / damp_value).astype(jnp.bfloat16)
    pre_all = lax.all_gather(pre_part, "blk", axis=1, tiled=True)
    partial_scores = jnp.einsum("qk,nk->qn", pre_all, train_rows, preferred_element_type=jnp.float32)
    scores = lax.psum_scatter(partial_scores, "col", scatter_dimension=0, tiled=True)
    return scores.astype(jnp.bfloat16)


def per_device(nb, pair, queries, factor, eigenvalues, damping, train_rows):
    rows, depth = queries.shape
    width = depth // nb
    fits = pair == 2 and width % 256 == 0 and eigenvalues.shape[0] % 512 == 0 and rows % 8 == 0 and factor.shape[1] % 16 == 0
    fits = fits and nb == 16
    if fits:
        return fused(nb, queries, factor, eigenvalues, damping, train_rows)
    return plain(queries, factor, eigenvalues, damping, train_rows)


def solution(mesh):
    in_specs = (P("blk", "col"), P("col", "blk"), P(), P(), P("blk", "col"))
    out_specs = P("col", "blk")
    body = functools.partial(per_device, mesh.shape["blk"], mesh.shape["col"])
    return jax.shard_map(
        body, mesh=mesh, in_specs=in_specs, out_specs=out_specs, check_vma=False
    )
```

```python
import functools

import jax
import jax.numpy as jnp
from jax import lax
from jax.experimental import pallas as pl
from jax.experimental.pallas import tpu as pltpu
from jax.sharding import PartitionSpec as P

MESH = pl.DeviceIdType.MESH
CONTRACT_LAST = (((1,), (1,)), ((), ()))


def fused_kernel(
    nb, queries, factor_t, eigenvalues, damping, train_rows, out,
    query_out, factor_out, query_in, factor_in, near_factor, train_in, part, pair_in, sum_in, scaled, near_scaled,
    terms, terms_out, terms_in, pre, total, total_in,
    train_sem, load_sem, query_send, query_recv, factor_send, factor_recv, near_send, near_recv,
    rows_send, rows_recv, sum_send, sum_recv, scaled_send, scaled_recv, terms_send, terms_recv,
    line_send, line_recv, far_send, side_send, side_recv, corner_send, corner_recv, pair_send, pair_recv,
):
    me = lax.axis_index("blk")
    side = lax.axis_index("col")
    rows, depth = queries.shape
    plane_size = 4
    line = nb // plane_size
    wide = depth // plane_size
    width = wide // line
    piece = width // 2
    every = nb * rows
    half = every // 2
    rank_slice = factor_t.shape[0]
    plane_rank = plane_size * rank_slice
    px, py, pz = lax.rem(me, 2), lax.rem(lax.div(me, 2), 2), lax.div(me, 4)
    z_low, z_high = lax.rem(pz, 2), lax.div(pz, 2)

    def flip(bit, yes):
        return 1 - bit if yes else bit

    def spot(k):
        return flip(px, k & 1) + 2 * flip(py, k & 2)

    def height_at(d):
        return flip(z_low, d & 1) + 2 * flip(z_high, d & 2)

    def chip(d, k):
        return height_at(d) * plane_size + spot(k)

    def span(index, size):
        return pl.ds(pl.multiple_of(index * size, size), size)

    def to_chip(source, target, send_sem, recv_sem, peer):
        return pltpu.make_async_remote_copy(
            src_ref=source, dst_ref=target, send_sem=send_sem, recv_sem=recv_sem,
            device_id={"blk": peer}, device_id_type=MESH,
        )

    def to_pair(source, target, index):
        return pltpu.make_async_remote_copy(
            src_ref=source, dst_ref=target,
            send_sem=pair_send.at[index], recv_sem=pair_recv.at[index],
            device_id={"col": 1 - side}, device_id_type=MESH,
        )

    def load_query(k):
        target = query_out.at[k - 1] if k else query_in.at[me]
        return pltpu.make_async_copy(queries.at[:, span(spot(k), wide)], target, load_sem.at[0, k])

    def load_factor(k):
        target = factor_out.at[k - 1] if k else factor_in.at[spot(0)]
        return pltpu.make_async_copy(factor_t.at[:, span(spot(k), wide)], target, load_sem.at[1, k])

    def query_copy(k, source):
        return to_chip(query_out.at[k - 1], query_in.at[source],
                       query_send.at[k - 1], query_recv.at[k - 1], chip(0, k))

    def factor_copy(k, source):
        return to_chip(factor_out.at[k - 1], factor_in.at[source],
                       factor_send.at[k - 1], factor_recv.at[k - 1], chip(0, k))

    def rows_copy(d, k, source):
        return to_chip(query_in.at[source], query_in.at[source],
                       rows_send.at[d - 1, k], rows_recv.at[d - 1, k], chip(d, 0))

    def sum_copy(k):
        return to_chip(part, sum_in.at[k - 1], sum_send.at[k - 1], sum_recv.at[k - 1], chip(0, k))

    def near_copy(part_index, k):
        columns = span(height_at(3 if part_index else 1), width)
        return to_chip(factor_in.at[spot(k), :, columns], near_factor.at[part_index, spot(k)],
                       near_send.at[part_index, k], near_recv.at[part_index, k], chip(1, 0))

    def scaled_copy(core):
        return pltpu.make_async_remote_copy(
            src_ref=scaled.at[0:every], dst_ref=near_scaled,
            send_sem=scaled_send.at[core], recv_sem=scaled_recv.at[0],
            device_id={"blk": chip(1, 0), "col": core}, device_id_type=MESH)

    def terms_copy(k):
        return to_chip(terms_out.at[k], terms_in.at[k], terms_send.at[k], terms_recv.at[k], chip(2, 0))

    def block(z, flip_x, flip_y):
        return z * plane_size + flip(py, flip_y) * 2 + flip(px, flip_x)

    def piece_of(index, k):
        return pre.at[index, :, pl.ds(k * piece, piece)]

    def line_copy(z, k, up):
        ref = piece_of(block(z, False, False), k)
        return to_chip(ref, ref, line_send.at[up, 2 * z + k], line_recv.at[2 * z + k],
                       me + (plane_size if up else -plane_size))

    next_x, next_y = chip(0, 1), chip(0, 2)

    def side_copy(z, k, along, incoming=False):
        ref = piece_of(block(z, incoming and along == 0, incoming and along == 1), k)
        return to_chip(ref, ref, side_send.at[along, 2 * z + k], side_recv.at[along, 2 * z + k],
                       next_y if along else next_x)

    def corner_copy(z, along, incoming=False):
        ref = piece_of(block(z, incoming or along == 1, incoming or along == 0), 1 - along)
        return to_chip(ref, ref, corner_send.at[along, z], corner_recv.at[along, z],
                       next_y if along else next_x)

    def train_copy(index):
        z, place = lax.div(index, plane_size), lax.rem(index, plane_size)
        return pltpu.make_async_copy(
            train_rows.at[:, span(place * line + z, width)], train_in.at[index], train_sem.at[index])

    for k in range(plane_size):
        load_query(k).start()
    for k in (3, 1, 2, 0):
        load_factor(k).start()

    barrier = pltpu.get_barrier_semaphore()
    for k in range(1, plane_size):
        pl.semaphore_signal(barrier, inc=1, device_id={"blk": chip(0, k)}, device_id_type=MESH)
    for d in range(1, line):
        pl.semaphore_signal(barrier, inc=1, device_id={"blk": chip(d, 0)}, device_id_type=MESH)
    pl.semaphore_signal(barrier, inc=1, device_id={"col": 1 - side}, device_id_type=MESH)
    pl.semaphore_signal(
        barrier, inc=1, device_id={"blk": chip(1, 0), "col": 1 - side}, device_id_type=MESH)
    pl.semaphore_wait(barrier, plane_size + line)

    for k in (3, 1, 2):
        load_query(k).wait()
        query_copy(k, me).start()
    for k in (3, 1, 2):
        load_factor(k).wait()
        factor_copy(k, spot(0)).start()
    load_query(0).wait()
    for d in (2, 3, 1):
        rows_copy(d, 0, me).start()
    load_factor(0).wait()
    for part_index in (1, 0):
        near_copy(part_index, 0).start()

    def start_train(k, carry):
        train_copy(lax.rem(me + nb - k, nb)).start()
        return carry
    lax.fori_loop(0, nb, start_train, 0)

    for k in range(1, plane_size):
        query_copy(k, chip(0, k)).wait_recv()
        for d in (2, 3, 1):
            rows_copy(d, k, chip(0, k)).start()
    for k in (1, 2, 3):
        factor_copy(k, spot(k)).wait_recv()
        for part_index in (1, 0):
            near_copy(part_index, k).start()
    for d in range(1, line):
        for k in range(plane_size):
            rows_copy(d, k, chip(d, k)).wait_recv()

    query_wide = query_in[...].astype(jnp.float32).reshape(every, wide).astype(jnp.bfloat16)
    partial_value = lax.dot_general(
        query_wide, factor_in[...].reshape(plane_rank, wide),
        CONTRACT_LAST, preferred_element_type=jnp.float32)
    part[...] = partial_value

    own_values = eigenvalues[:, span(pz, plane_rank)]
    weights = own_values / (own_values + damping[0])

    @pl.when(side == 0)
    def _():
        to_pair(part, pair_in, 0).start()
        to_pair(scaled, scaled, 1).wait_recv()
        to_pair(part, pair_in, 0).wait_send()

    @pl.when(side == 1)
    def _():
        to_pair(part, pair_in, 0).wait_recv()
        part[...] = part[...] + pair_in[...]
        for k in (3, 1, 2):
            sum_copy(k).start()
        for k in (1, 2, 3):
            sum_copy(k).wait_recv()
        whole = ((part[...] + sum_in[0]) + (sum_in[1] + sum_in[2])) * weights
        first = whole.astype(jnp.bfloat16)
        scaled[0:every] = first
        scaled[every:2 * every] = (whole - first.astype(jnp.float32)).astype(jnp.bfloat16)
        scaled_copy(0).start()
        to_pair(scaled, scaled, 1).start()
        scaled_copy(1).start()

    parts = ((1, 0), (1, 1), (0, 0), (0, 1))

    def product(values, factor_part):
        return jnp.dot(values, factor_part.reshape(plane_rank, piece),
                       preferred_element_type=jnp.float32)

    for part_index, k in parts:
        columns = span(2 * height_at(2 * part_index) + k, piece)
        both = product(scaled[...], factor_in[:, :, columns])
        terms[part_index, k] = both[:every] + both[every:]
    for part_index in (1, 0):
        for k in range(plane_size):
            near_copy(part_index, k).wait_recv()
    scaled_copy(0).wait_recv()
    for part_index, k in parts:
        near_part = near_factor[part_index, :, :, k * piece:(k + 1) * piece]
        whole = terms[part_index, k] + product(near_scaled[...], near_part)
        if part_index:
            terms_out[k] = whole.astype(jnp.bfloat16)
            terms_copy(k).start()
        else:
            terms[part_index, k] = whole
    inverse = 1.0 / damping[0]

    def finish_own(k):
        terms_copy(k).wait_recv()
        whole = terms[0, k] + terms_in[k].astype(jnp.float32)
        start = pl.multiple_of(pz * width + k * piece, piece)
        own = query_in[:, :, pl.ds(start, piece)].astype(jnp.float32).reshape(every, piece)
        pre[me, :, k * piece:(k + 1) * piece] = ((own - whole) * inverse).astype(jnp.bfloat16)

    def scores_of(index):
        train_copy(index).wait()
        return lax.dot_general(
            pre[index], train_in[index], CONTRACT_LAST, preferred_element_type=jnp.float32)

    def height(i):
        mirror = lax.div(pz, line // 2)
        near = pz + mirror * (line - 1 - 2 * pz)
        v = near + i * (1 - 2 * near) if i < 2 else i
        return v + mirror * (line - 1 - 2 * v)

    def pass_on(z, k):
        @pl.when((z <= pz) & (pz < line - 1))
        def _():
            line_copy(z, k, 1).start()

        @pl.when((z >= pz) & (pz > 0))
        def _():
            line_copy(z, k, 0).start()

    total[...] = jnp.zeros_like(total)
    def add_scores(z, flip_x, flip_y):
        total[...] += scores_of(block(z, flip_x, flip_y))

    direct_line, direct_corner = (True, False), (((3, 1),), ())

    def for_cores(chosen, body, otherwise=None):
        if chosen[0] == chosen[1]:
            if chosen[0]:
                body()
            elif otherwise:
                otherwise()
            return
        pl.when(side == (1 if chosen[1] else 0))(body)
        if otherwise:
            pl.when(side == (0 if chosen[1] else 1))(otherwise)

    def far_copy(d, k):
        ref = piece_of(me, k)
        return to_chip(ref, ref, far_send.at[d - 1, k], line_recv.at[2 * pz + k], chip(d, 0))

    def diagonal_copy(z, k):
        ref = piece_of(block(z, False, False), k)
        return to_chip(ref, ref, corner_send.at[1 - k, z], corner_recv.at[1 - k, z], chip(0, 3))

    def at_corner(i, k):
        return tuple((i, k) in direct_corner[core] for core in range(2))

    def start_line(i, k):
        def direct():
            if i == 0:
                for d in (3, 2, 1):
                    far_copy(d, k).start()
        for_cores(direct_line, direct, lambda: pass_on(height(i), k))

    def line_sent(i, k):
        z = height(i)

        def direct():
            if i == 0:
                for d in (3, 2, 1):
                    far_copy(d, k).wait_send()

        def relayed():
            @pl.when((z <= pz) & (pz < line - 1))
            def _():
                line_copy(z, k, 1).wait_send()

            @pl.when((z >= pz) & (pz > 0))
            def _():
                line_copy(z, k, 0).wait_send()
        for_cores(direct_line, direct, relayed)

    def arrive(i, k):
        z = height(i)
        if i > 0:
            line_copy(z, k, 1).wait_recv()
        else:
            finish_own(k)
        start_line(i, k)
        for_cores(at_corner(i, k), lambda: diagonal_copy(z, k).start())
        side_copy(z, k, k).start()

    def spread(i, k):
        side_copy(height(i), k, 1 - k).start()

    def turn(i, k):
        z = height(i)
        side_copy(z, k, k, True).wait_recv()
        if i != 1:
            for_cores(at_corner(i, k), lambda: None, lambda: corner_copy(z, 1 - k).start())

    def add_own(i):
        add_scores(height(i), False, False)

    def add_side(i, along):
        z = height(i)
        side_copy(z, 1 - along, along, True).wait_recv()
        add_scores(z, along == 0, along == 1)

    def share_copy(k):
        ref = piece_of(block(pz, True, True), k)
        return to_chip(ref, ref, corner_send.at[1 - k, height(1)], corner_recv.at[1 - k, pz], chip(1, 0))

    def share():
        for k in range(2):
            corner_copy(pz, 1 - k, True).wait_recv()
            share_copy(k).start()

    def add_corner(i):
        z = height(i)
        if i > 0:
            for along in range(2):
                corner_copy(z, along, True).wait_recv()
        add_scores(z, True, True)

    arrive(0, 0)
    spread(0, 0)
    arrive(0, 1)
    spread(0, 1)
    add_own(0)
    arrive(1, 0)
    spread(1, 0)
    arrive(1, 1)
    spread(1, 1)
    turn(0, 0)
    add_own(1)
    arrive(2, 0)
    spread(2, 0)
    turn(0, 1)
    add_side(0, 0)
    add_side(0, 1)
    arrive(2, 1)
    spread(2, 1)
    turn(1, 0)
    add_own(2)
    arrive(3, 0)
    spread(3, 0)
    turn(1, 1)
    add_side(1, 0)
    add_side(1, 1)
    share()
    arrive(3, 1)
    spread(3, 1)
    turn(2, 0)
    add_own(3)
    turn(2, 1)
    add_side(2, 0)
    add_side(2, 1)
    add_corner(0)
    turn(3, 0)
    turn(3, 1)
    add_side(3, 0)
    add_side(3, 1)
    add_corner(1)
    add_corner(2)
    add_corner(3)
    other_rows = pl.ds(pl.multiple_of((1 - side) * half, half), half)
    own_rows = pl.ds(pl.multiple_of(side * half, half), half)
    last = to_pair(total.at[other_rows], total_in, 2)
    last.start()

    for k in range(1, plane_size):
        query_copy(k, me).wait_send()
        factor_copy(k, spot(0)).wait_send()
    for d in range(1, line):
        for k in range(plane_size):
            rows_copy(d, k, chip(0, k)).wait_send()
    for k in range(plane_size):
        for part_index in range(2):
            near_copy(part_index, k).wait_send()
    for k in range(2):
        terms_copy(k).wait_send()

    @pl.when(side == 1)
    def _():
        for k in range(1, plane_size):
            sum_copy(k).wait_send()
        to_pair(scaled, scaled, 1).wait_send()
        for core in range(2):
            scaled_copy(core).wait_send()

    for i in range(line):
        z = height(i)
        for k in range(2):
            line_sent(i, k)
            for along in range(2):
                side_copy(z, k, along).wait_send()
        for along in range(2):
            corner_copy(z, along).wait_send()
    last.wait()
    out[...] = (total[own_rows, :] + total_in[...]).astype(out.dtype)


def fused(nb, queries, factor, eigenvalues, damping, train_rows):
    rows, depth = queries.shape
    rank_slice = factor.shape[1]
    plane_size = 4
    line = nb // plane_size
    wide = depth // plane_size
    width = wide // line
    every = nb * rows
    train = train_rows.shape[0]
    plane_rank = plane_size * rank_slice
    anywhere = pl.BlockSpec(memory_space=pl.ANY)
    vmem = pl.BlockSpec(memory_space=pltpu.VMEM)
    dma = pltpu.SemaphoreType.DMA
    f32, bf16 = jnp.float32, jnp.bfloat16
    return pl.pallas_call(
        functools.partial(fused_kernel, nb),
        out_shape=jax.ShapeDtypeStruct((every // 2, train), bf16),
        in_specs=[anywhere, anywhere, vmem, pl.BlockSpec(memory_space=pltpu.SMEM), anywhere],
        out_specs=vmem,
        scratch_shapes=[
            pltpu.VMEM((plane_size - 1, rows, wide), bf16),
            pltpu.VMEM((plane_size - 1, rank_slice, wide), bf16),
            pltpu.VMEM((nb, rows, wide), bf16),
            pltpu.VMEM((plane_size, rank_slice, wide), bf16),
            pltpu.VMEM((2, plane_size, rank_slice, width), bf16),
            pltpu.VMEM((nb, train, width), bf16),
            pltpu.VMEM((every, plane_rank), f32),
            pltpu.VMEM((every, plane_rank), f32),
            pltpu.VMEM((plane_size - 1, every, plane_rank), f32),
            pltpu.VMEM((2 * every, plane_rank), bf16),
            pltpu.VMEM((every, plane_rank), bf16),
            pltpu.VMEM((2, 2, every, width // 2), f32),
            pltpu.VMEM((2, every, width // 2), bf16),
            pltpu.VMEM((2, every, width // 2), bf16),
            pltpu.VMEM((nb, every, width), bf16),
            pltpu.VMEM((every, train), f32),
            pltpu.VMEM((every // 2, train), f32),
            dma((nb,)), dma((2, plane_size)),
            dma((plane_size - 1,)), dma((plane_size - 1,)),
            dma((plane_size - 1,)), dma((plane_size - 1,)),
            dma((2, plane_size)), dma((2, plane_size)),
            dma((line - 1, plane_size)), dma((line - 1, plane_size)),
            dma((plane_size - 1,)), dma((plane_size - 1,)),
            dma((2,)), dma((1,)), dma((2,)), dma((2,)),
            dma((2, 2 * line)), dma((2 * line,)), dma((line - 1, 2)), dma((2, 2 * line)), dma((2, 2 * line)),
            dma((2, line)), dma((2, line)), dma((3,)), dma((3,)),
        ],
        compiler_params=pltpu.CompilerParams(
            collective_id=0, has_side_effects=True, vmem_limit_bytes=55040 * 1024),
    )(queries, factor.T, eigenvalues[None, :], damping, train_rows)


def plain(queries, factor, eigenvalues, damping, train_rows):
    damp_value = damping[0]
    weights = eigenvalues / (eigenvalues + damp_value)
    query_part = lax.all_to_all(queries, "blk", split_axis=1, concat_axis=0, tiled=True)
    factor_part = lax.all_to_all(factor, "blk", split_axis=0, concat_axis=1, tiled=True)
    partial_value = jnp.dot(query_part, factor_part, preferred_element_type=jnp.float32)
    coefficient = lax.psum(partial_value, ("blk", "col"))
    scaled = coefficient * weights[None, :]
    correction = jnp.dot(scaled, factor_part.astype(jnp.float32).T, precision=lax.Precision.HIGHEST)
    pre_part = ((query_part.astype(jnp.float32) - correction) / damp_value).astype(jnp.bfloat16)
    pre_all = lax.all_gather(pre_part, "blk", axis=1, tiled=True)
    partial_scores = jnp.einsum("qk,nk->qn", pre_all, train_rows, preferred_element_type=jnp.float32)
    scores = lax.psum_scatter(partial_scores, "col", scatter_dimension=0, tiled=True)
    return scores.astype(jnp.bfloat16)


def per_device(nb, pair, queries, factor, eigenvalues, damping, train_rows):
    rows, depth = queries.shape
    width = depth // nb
    fits = pair == 2 and width % 256 == 0 and eigenvalues.shape[0] % 512 == 0 and rows % 8 == 0 and factor.shape[1] % 16 == 0
    fits = fits and nb == 16
    if fits:
        return fused(nb, queries, factor, eigenvalues, damping, train_rows)
    return plain(queries, factor, eigenvalues, damping, train_rows)


def solution(mesh):
    in_specs = (P("blk", "col"), P("col", "blk"), P(), P(), P("blk", "col"))
    out_specs = P("col", "blk")
    body = functools.partial(per_device, mesh.shape["blk"], mesh.shape["col"])
    return jax.shard_map(
        body, mesh=mesh, in_specs=in_specs, out_specs=out_specs, check_vma=False
    )
```

```python
import functools

import jax
import jax.numpy as jnp
from jax import lax
from jax.experimental import pallas as pl
from jax.experimental.pallas import tpu as pltpu
from jax.sharding import PartitionSpec as P

MESH = pl.DeviceIdType.MESH
CONTRACT_LAST = (((1,), (1,)), ((), ()))


def fused_kernel(
    nb, queries, factor_t, eigenvalues, damping, train_rows, out,
    query_out, factor_out, query_in, factor_in, near_factor, train_in, part, pair_in, sum_out, sum_in, scaled, near_scaled,
    terms, terms_out, terms_in, beside_out, beside_in, pre, total, total_in,
    train_sem, load_sem, query_send, query_recv, factor_send, factor_recv, near_send, near_recv,
    rows_send, rows_recv, sum_send, sum_recv, scaled_send, scaled_recv, terms_send, terms_recv, beside_send, beside_recv,
    line_send, line_recv, far_send, side_send, side_recv, corner_send, corner_recv, pair_send, pair_recv,
):
    me = lax.axis_index("blk")
    side = lax.axis_index("col")
    rows, depth = queries.shape
    plane_size = 4
    line = nb // plane_size
    wide = depth // plane_size
    width = wide // line
    piece = width // 2
    every = nb * rows
    half = every // 2
    rank_slice = factor_t.shape[0]
    plane_rank = plane_size * rank_slice
    px, py, pz = lax.rem(me, 2), lax.rem(lax.div(me, 2), 2), lax.div(me, 4)
    z_low, z_high = lax.rem(pz, 2), lax.div(pz, 2)

    def flip(bit, yes):
        return 1 - bit if yes else bit

    def spot(k):
        return flip(px, k & 1) + 2 * flip(py, k & 2)

    def height_at(d):
        return flip(z_low, d & 1) + 2 * flip(z_high, d & 2)

    def chip(d, k):
        return height_at(d) * plane_size + spot(k)

    def span(index, size):
        return pl.ds(pl.multiple_of(index * size, size), size)

    def to_chip(source, target, send_sem, recv_sem, peer):
        return pltpu.make_async_remote_copy(
            src_ref=source, dst_ref=target, send_sem=send_sem, recv_sem=recv_sem,
            device_id={"blk": peer}, device_id_type=MESH,
        )

    def to_pair(source, target, index):
        return pltpu.make_async_remote_copy(
            src_ref=source, dst_ref=target,
            send_sem=pair_send.at[index], recv_sem=pair_recv.at[index],
            device_id={"col": 1 - side}, device_id_type=MESH,
        )

    def load_query(k):
        target = query_out.at[k - 1] if k else query_in.at[me]
        return pltpu.make_async_copy(queries.at[:, span(spot(k), wide)], target, load_sem.at[0, k])

    def load_factor(k):
        target = factor_out.at[k - 1] if k else factor_in.at[spot(0)]
        return pltpu.make_async_copy(factor_t.at[:, span(spot(k), wide)], target, load_sem.at[1, k])

    def query_copy(k, source):
        return to_chip(query_out.at[k - 1], query_in.at[source],
                       query_send.at[k - 1], query_recv.at[k - 1], chip(0, k))

    def factor_copy(k, source):
        return to_chip(factor_out.at[k - 1], factor_in.at[source],
                       factor_send.at[k - 1], factor_recv.at[k - 1], chip(0, k))

    def rows_copy(d, k, source):
        return to_chip(query_in.at[source], query_in.at[source],
                       rows_send.at[d - 1, k], rows_recv.at[d - 1, k], chip(d, 0))

    def sum_copy(k):
        return to_chip(sum_out, sum_in.at[k - 1], sum_send.at[k - 1], sum_recv.at[k - 1], chip(0, k))

    def near_copy(part_index, k):
        columns = span(height_at(3 if part_index else 1), width)
        return to_chip(factor_in.at[spot(k), :, columns], near_factor.at[part_index, spot(k)],
                       near_send.at[part_index, k], near_recv.at[part_index, k], chip(1, 0))

    def scaled_copy(core):
        return pltpu.make_async_remote_copy(
            src_ref=scaled.at[0:every], dst_ref=near_scaled,
            send_sem=scaled_send.at[core], recv_sem=scaled_recv.at[0],
            device_id={"blk": chip(1, 0), "col": core}, device_id_type=MESH)

    def beside_copy(k):
        return to_chip(beside_out.at[k], beside_in.at[k], beside_send.at[k], beside_recv.at[k], chip(1, 0))

    def terms_copy(k):
        return to_chip(terms_out.at[k], terms_in.at[k], terms_send.at[k], terms_recv.at[k], chip(2, 0))

    def block(z, flip_x, flip_y):
        return z * plane_size + flip(py, flip_y) * 2 + flip(px, flip_x)

    def piece_of(index, k):
        return pre.at[index, :, pl.ds(k * piece, piece)]

    def line_copy(z, k, up):
        ref = piece_of(block(z, False, False), k)
        return to_chip(ref, ref, line_send.at[up, 2 * z + k], line_recv.at[2 * z + k],
                       me + (plane_size if up else -plane_size))

    next_x, next_y = chip(0, 1), chip(0, 2)

    def side_copy(z, k, along, incoming=False):
        ref = piece_of(block(z, incoming and along == 0, incoming and along == 1), k)
        return to_chip(ref, ref, side_send.at[along, 2 * z + k], side_recv.at[along, 2 * z + k],
                       next_y if along else next_x)

    def corner_copy(z, along, incoming=False):
        ref = piece_of(block(z, incoming or along == 1, incoming or along == 0), 1 - along)
        return to_chip(ref, ref, corner_send.at[along, z], corner_recv.at[along, z],
                       next_y if along else next_x)

    def train_copy(index):
        z, place = lax.div(index, plane_size), lax.rem(index, plane_size)
        return pltpu.make_async_copy(
            train_rows.at[:, span(place * line + z, width)], train_in.at[index], train_sem.at[index])

    for k in range(plane_size):
        load_query(k).start()
    for k in (3, 1, 2, 0):
        load_factor(k).start()

    barrier = pltpu.get_barrier_semaphore()
    for k in range(1, plane_size):
        pl.semaphore_signal(barrier, inc=1, device_id={"blk": chip(0, k)}, device_id_type=MESH)
    for d in range(1, line):
        pl.semaphore_signal(barrier, inc=1, device_id={"blk": chip(d, 0)}, device_id_type=MESH)
    pl.semaphore_signal(barrier, inc=1, device_id={"col": 1 - side}, device_id_type=MESH)
    pl.semaphore_signal(
        barrier, inc=1, device_id={"blk": chip(1, 0), "col": 1 - side}, device_id_type=MESH)
    pl.semaphore_wait(barrier, plane_size + line)

    for k in (3, 1, 2):
        load_query(k).wait()
        query_copy(k, me).start()
    for k in (3, 1, 2):
        load_factor(k).wait()
        factor_copy(k, spot(0)).start()
    load_query(0).wait()
    for d in (2, 3, 1):
        rows_copy(d, 0, me).start()
    load_factor(0).wait()
    for part_index in (1,):
        near_copy(part_index, 0).start()

    def start_train(k, carry):
        train_copy(lax.rem(me + nb - k, nb)).start()
        return carry
    lax.fori_loop(0, nb, start_train, 0)

    for k in range(1, plane_size):
        query_copy(k, chip(0, k)).wait_recv()
        for d in (2, 3, 1):
            rows_copy(d, k, chip(0, k)).start()
    for d in range(1, line):
        for k in range(plane_size):
            rows_copy(d, k, chip(d, k)).wait_recv()
    query_wide = query_in[...].astype(jnp.float32).reshape(every, wide).astype(jnp.bfloat16)
    for k in (1, 2, 3):
        factor_copy(k, spot(k)).wait_recv()
        for part_index in (1,):
            near_copy(part_index, k).start()
    partial_value = lax.dot_general(
        query_wide, factor_in[...].reshape(plane_rank, wide),
        CONTRACT_LAST, preferred_element_type=jnp.float32)
    part[...] = partial_value

    own_values = eigenvalues[:, span(pz, plane_rank)]
    weights = own_values / (own_values + damping[0])

    @pl.when(side == 0)
    def _():
        to_pair(part, pair_in, 0).start()
        to_pair(scaled, scaled, 1).wait_recv()
        to_pair(part, pair_in, 0).wait_send()

    @pl.when(side == 1)
    def _():
        to_pair(part, pair_in, 0).wait_recv()
        part[...] = part[...] + pair_in[...]
        sum_out[...] = part[...].astype(jnp.bfloat16)
        for k in (3, 1, 2):
            sum_copy(k).start()
        for k in (1, 2, 3):
            sum_copy(k).wait_recv()
        arrived = [sum_in[k].astype(jnp.float32) for k in range(3)]
        whole = ((part[...] + arrived[0]) + (arrived[1] + arrived[2])) * weights
        first = whole.astype(jnp.bfloat16)
        scaled[0:every] = first
        scaled[every:2 * every] = (whole - first.astype(jnp.float32)).astype(jnp.bfloat16)
        scaled_copy(0).start()
        to_pair(scaled, scaled, 1).start()
        scaled_copy(1).start()

    def product(values, factor_part):
        return jnp.dot(values, factor_part.reshape(plane_rank, piece),
                       preferred_element_type=jnp.float32)

    def plane_terms(d, k):
        both = product(scaled[...], factor_in[:, :, span(2 * height_at(d) + k, piece)])
        return both[:every] + both[every:]

    for k in range(2):
        beside_out[k] = plane_terms(1, k).astype(jnp.bfloat16)
        beside_copy(k).start()
    for k in range(2):
        terms[1, k] = plane_terms(2, k)
    for k in range(plane_size):
        near_copy(1, k).wait_recv()
    scaled_copy(0).wait_recv()
    for k in range(2):
        near_part = near_factor[1, :, :, k * piece:(k + 1) * piece]
        terms_out[k] = (terms[1, k] + product(near_scaled[...], near_part)).astype(jnp.bfloat16)
        terms_copy(k).start()
    for k in range(2):
        terms[0, k] = plane_terms(0, k)
    inverse = 1.0 / damping[0]

    def finish_own(k):
        terms_copy(k).wait_recv()
        beside_copy(k).wait_recv()
        whole = terms[0, k] + (terms_in[k].astype(jnp.float32) + beside_in[k].astype(jnp.float32))
        start = pl.multiple_of(pz * width + k * piece, piece)
        own = query_in[:, :, pl.ds(start, piece)].astype(jnp.float32).reshape(every, piece)
        pre[me, :, k * piece:(k + 1) * piece] = ((own - whole) * inverse).astype(jnp.bfloat16)

    def scores_of(index):
        train_copy(index).wait()
        return lax.dot_general(
            pre[index], train_in[index], CONTRACT_LAST, preferred_element_type=jnp.float32)

    def height(i):
        mirror = lax.div(pz, line // 2)
        near = pz + mirror * (line - 1 - 2 * pz)
        v = near + i * (1 - 2 * near) if i < 2 else i
        return v + mirror * (line - 1 - 2 * v)

    def pass_on(z, k):
        @pl.when((z <= pz) & (pz < line - 1))
        def _():
            line_copy(z, k, 1).start()

        @pl.when((z >= pz) & (pz > 0))
        def _():
            line_copy(z, k, 0).start()

    total[...] = jnp.zeros_like(total)
    def add_scores(z, flip_x, flip_y):
        total[...] += scores_of(block(z, flip_x, flip_y))

    direct_line, direct_corner = (True, False), (((3, 1),), ())

    def for_cores(chosen, body, otherwise=None):
        if chosen[0] == chosen[1]:
            if chosen[0]:
                body()
            elif otherwise:
                otherwise()
            return
        pl.when(side == (1 if chosen[1] else 0))(body)
        if otherwise:
            pl.when(side == (0 if chosen[1] else 1))(otherwise)

    def far_copy(d, k):
        ref = piece_of(me, k)
        return to_chip(ref, ref, far_send.at[d - 1, k], line_recv.at[2 * pz + k], chip(d, 0))

    def diagonal_copy(z, k):
        ref = piece_of(block(z, False, False), k)
        return to_chip(ref, ref, corner_send.at[1 - k, z], corner_recv.at[1 - k, z], chip(0, 3))

    def at_corner(i, k):
        return tuple((i, k) in direct_corner[core] for core in range(2))

    def start_line(i, k):
        def direct():
            if i == 0:
                for d in (3, 2, 1):
                    far_copy(d, k).start()
        for_cores(direct_line, direct, lambda: pass_on(height(i), k))

    def line_sent(i, k):
        z = height(i)

        def direct():
            if i == 0:
                for d in (3, 2, 1):
                    far_copy(d, k).wait_send()

        def relayed():
            @pl.when((z <= pz) & (pz < line - 1))
            def _():
                line_copy(z, k, 1).wait_send()

            @pl.when((z >= pz) & (pz > 0))
            def _():
                line_copy(z, k, 0).wait_send()
        for_cores(direct_line, direct, relayed)

    def arrive(i, k):
        z = height(i)
        if i > 0:
            line_copy(z, k, 1).wait_recv()
        else:
            finish_own(k)
        start_line(i, k)
        for_cores(at_corner(i, k), lambda: diagonal_copy(z, k).start())
        side_copy(z, k, k).start()

    def spread(i, k):
        side_copy(height(i), k, 1 - k).start()

    def turn(i, k):
        z = height(i)
        side_copy(z, k, k, True).wait_recv()
        if i != 1:
            for_cores(at_corner(i, k), lambda: None, lambda: corner_copy(z, 1 - k).start())

    def add_own(i):
        add_scores(height(i), False, False)

    def add_side(i, along):
        z = height(i)
        side_copy(z, 1 - along, along, True).wait_recv()
        add_scores(z, along == 0, along == 1)

    def share_copy(k):
        ref = piece_of(block(pz, True, True), k)
        return to_chip(ref, ref, corner_send.at[1 - k, height(1)], corner_recv.at[1 - k, pz], chip(1, 0))

    def share():
        for k in range(2):
            corner_copy(pz, 1 - k, True).wait_recv()
            share_copy(k).start()

    def add_corner(i):
        z = height(i)
        if i > 0:
            for along in range(2):
                corner_copy(z, along, True).wait_recv()
        add_scores(z, True, True)

    arrive(0, 0)
    spread(0, 0)
    arrive(0, 1)
    spread(0, 1)
    add_own(0)
    arrive(1, 0)
    spread(1, 0)
    arrive(1, 1)
    spread(1, 1)
    turn(0, 0)
    add_own(1)
    arrive(2, 0)
    spread(2, 0)
    turn(0, 1)
    add_side(0, 0)
    add_side(0, 1)
    arrive(2, 1)
    spread(2, 1)
    turn(1, 0)
    add_own(2)
    arrive(3, 0)
    spread(3, 0)
    turn(1, 1)
    add_side(1, 0)
    add_side(1, 1)
    share()
    arrive(3, 1)
    spread(3, 1)
    turn(2, 0)
    add_own(3)
    turn(2, 1)
    add_side(2, 0)
    add_side(2, 1)
    add_corner(0)
    turn(3, 0)
    turn(3, 1)
    add_side(3, 0)
    add_side(3, 1)
    add_corner(1)
    add_corner(2)
    add_corner(3)
    other_rows = pl.ds(pl.multiple_of((1 - side) * half, half), half)
    own_rows = pl.ds(pl.multiple_of(side * half, half), half)
    last = to_pair(total.at[other_rows], total_in, 2)
    last.start()

    for k in range(1, plane_size):
        query_copy(k, me).wait_send()
        factor_copy(k, spot(0)).wait_send()
    for d in range(1, line):
        for k in range(plane_size):
            rows_copy(d, k, chip(0, k)).wait_send()
    for k in range(plane_size):
        near_copy(1, k).wait_send()
    for k in range(2):
        terms_copy(k).wait_send()
        beside_copy(k).wait_send()

    @pl.when(side == 1)
    def _():
        for k in range(1, plane_size):
            sum_copy(k).wait_send()
        to_pair(scaled, scaled, 1).wait_send()
        for core in range(2):
            scaled_copy(core).wait_send()

    for i in range(line):
        z = height(i)
        for k in range(2):
            line_sent(i, k)
            for along in range(2):
                side_copy(z, k, along).wait_send()
        for along in range(2):
            corner_copy(z, along).wait_send()
    last.wait()
    out[...] = (total[own_rows, :] + total_in[...]).astype(out.dtype)


def fused(nb, queries, factor, eigenvalues, damping, train_rows):
    rows, depth = queries.shape
    rank_slice = factor.shape[1]
    plane_size = 4
    line = nb // plane_size
    wide = depth // plane_size
    width = wide // line
    every = nb * rows
    train = train_rows.shape[0]
    plane_rank = plane_size * rank_slice
    anywhere = pl.BlockSpec(memory_space=pl.ANY)
    vmem = pl.BlockSpec(memory_space=pltpu.VMEM)
    dma = pltpu.SemaphoreType.DMA
    f32, bf16 = jnp.float32, jnp.bfloat16
    return pl.pallas_call(
        functools.partial(fused_kernel, nb),
        out_shape=jax.ShapeDtypeStruct((every // 2, train), bf16),
        in_specs=[anywhere, anywhere, vmem, pl.BlockSpec(memory_space=pltpu.SMEM), anywhere],
        out_specs=vmem,
        scratch_shapes=[
            pltpu.VMEM((plane_size - 1, rows, wide), bf16),
            pltpu.VMEM((plane_size - 1, rank_slice, wide), bf16),
            pltpu.VMEM((nb, rows, wide), bf16),
            pltpu.VMEM((plane_size, rank_slice, wide), bf16),
            pltpu.VMEM((2, plane_size, rank_slice, width), bf16),
            pltpu.VMEM((nb, train, width), bf16),
            pltpu.VMEM((every, plane_rank), f32),
            pltpu.VMEM((every, plane_rank), f32),
            pltpu.VMEM((every, plane_rank), bf16),
            pltpu.VMEM((plane_size - 1, every, plane_rank), bf16),
            pltpu.VMEM((2 * every, plane_rank), bf16),
            pltpu.VMEM((every, plane_rank), bf16),
            pltpu.VMEM((2, 2, every, width // 2), f32),
            pltpu.VMEM((2, every, width // 2), bf16),
            pltpu.VMEM((2, every, width // 2), bf16),
            pltpu.VMEM((2, every, width // 2), bf16),
            pltpu.VMEM((2, every, width // 2), bf16),
            pltpu.VMEM((nb, every, width), bf16),
            pltpu.VMEM((every, train), f32),
            pltpu.VMEM((every // 2, train), f32),
            dma((nb,)), dma((2, plane_size)),
            dma((plane_size - 1,)), dma((plane_size - 1,)),
            dma((plane_size - 1,)), dma((plane_size - 1,)),
            dma((2, plane_size)), dma((2, plane_size)),
            dma((line - 1, plane_size)), dma((line - 1, plane_size)),
            dma((plane_size - 1,)), dma((plane_size - 1,)),
            dma((2,)), dma((1,)), dma((2,)), dma((2,)), dma((2,)), dma((2,)),
            dma((2, 2 * line)), dma((2 * line,)), dma((line - 1, 2)), dma((2, 2 * line)), dma((2, 2 * line)),
            dma((2, line)), dma((2, line)), dma((3,)), dma((3,)),
        ],
        compiler_params=pltpu.CompilerParams(
            collective_id=0, has_side_effects=True, vmem_limit_bytes=55040 * 1024),
    )(queries, factor.T, eigenvalues[None, :], damping, train_rows)


def plain(queries, factor, eigenvalues, damping, train_rows):
    damp_value = damping[0]
    weights = eigenvalues / (eigenvalues + damp_value)
    query_part = lax.all_to_all(queries, "blk", split_axis=1, concat_axis=0, tiled=True)
    factor_part = lax.all_to_all(factor, "blk", split_axis=0, concat_axis=1, tiled=True)
    partial_value = jnp.dot(query_part, factor_part, preferred_element_type=jnp.float32)
    coefficient = lax.psum(partial_value, ("blk", "col"))
    scaled = coefficient * weights[None, :]
    correction = jnp.dot(scaled, factor_part.astype(jnp.float32).T, precision=lax.Precision.HIGHEST)
    pre_part = ((query_part.astype(jnp.float32) - correction) / damp_value).astype(jnp.bfloat16)
    pre_all = lax.all_gather(pre_part, "blk", axis=1, tiled=True)
    partial_scores = jnp.einsum("qk,nk->qn", pre_all, train_rows, preferred_element_type=jnp.float32)
    scores = lax.psum_scatter(partial_scores, "col", scatter_dimension=0, tiled=True)
    return scores.astype(jnp.bfloat16)


def per_device(nb, pair, queries, factor, eigenvalues, damping, train_rows):
    rows, depth = queries.shape
    width = depth // nb
    fits = pair == 2 and width % 256 == 0 and eigenvalues.shape[0] % 512 == 0 and rows % 8 == 0 and factor.shape[1] % 16 == 0
    fits = fits and nb == 16
    if fits:
        return fused(nb, queries, factor, eigenvalues, damping, train_rows)
    return plain(queries, factor, eigenvalues, damping, train_rows)


def solution(mesh):
    in_specs = (P("blk", "col"), P("col", "blk"), P(), P(), P("blk", "col"))
    out_specs = P("col", "blk")
    body = functools.partial(per_device, mesh.shape["blk"], mesh.shape["col"])
    return jax.shard_map(
        body, mesh=mesh, in_specs=in_specs, out_specs=out_specs, check_vma=False
    )
```
